32 devices in a mesh: blk: 8 (over z, x), rows: 4 (over y, core).
Axes of the slice: x: 2, y: 2, z: 4, core: 2. Of those that a mesh axis runs over, the one named last changes fastest.
Arguments:
- features: bfloat16 [8192, 2048], P(('blk', 'rows')), may hold values from -6 to 6
- head_weight: bfloat16 [2048, 768], replicated, may hold values from -0.0048828125 to 0.0048828125
- labels: int32 [8192], P(('blk', 'rows')), may hold values from 0 to 11317
- pos_index: int32 [8192, 3], P(('blk', 'rows')), may hold values from 0 to 1023
- pair_mask: int32 [8, 3], P('blk'), may hold values from 0 to 1, as said below
- loss_weight: float32 [8192], P(('blk', 'rows')), may hold values from 0.25 to 1
Outputs:
- anchor_loss: float32 [8192], P(('blk', 'rows'))
- weight_grad: float32 [2048, 768], P(('blk', 'rows'))
The draws below stay inside these ranges and needn't reach their ends.
Inputs may be any that keep to these rules, and one draw needn't show every extreme that they name: `pair_mask`: entry [t, s] is 1 where anchor tile t scores the rows of tile (t - s) mod 8, else 0. The rows of tiles 0 to 2 and of tile 8 - 1 are all ones.
All inputs are finite; a program needn't handle non-finite values.
Results may differ from the reference program's by a relative error of at most 0.0034.
Values may be sent and summed in bfloat16 or wider, within the bound.
A program may use at most 128 MiB of HBM per device.

```python
import math
import jax
import jax.numpy as jnp
import numpy as np
from jax import lax

D = 768
F = 2048
POSITIVES = 3
WIN = 2
CLASSES = 11318
BAND = 3
TILE = 1024
BATCH = 8192
N_BLK = 8


def draw_pair_mask(key, part):
    level_key, score_key = jax.random.split(jax.random.fold_in(key, 17))
    levels = jax.random.randint(level_key, (N_BLK, 1), 1, BAND + 1)
    scores = jax.random.randint(score_key, (N_BLK, BAND), 0, BAND * BAND * BAND)
    base = (scores < levels * levels * levels).astype(jnp.int32)
    tile_ids = jnp.arange(N_BLK, dtype=jnp.int32)[:, None]
    forced = (tile_ids <= WIN) | (tile_ids >= N_BLK - 1)
    return jnp.where(forced, jnp.ones_like(base), base).astype(jnp.int32)


def plant(drawn, rng, low, largest):
    shape = drawn.shape
    spot = [jax.random.randint(jax.random.fold_in(rng, axis), (), 0, shape[axis]) for axis in range(len(shape))]
    drawn = drawn.at[tuple(spot)].set(low)
    longest = shape.index(max(shape))
    spot[longest] = (spot[longest] + 1) % shape[longest]
    return drawn.at[tuple(spot)].set(largest)


def spiked(array, own_key, source, target, blocks, factor):
    def block_of(axis_at):
        return (jnp.arange(array.shape[axis_at]) // (array.shape[axis_at] // blocks)).reshape((-1,) + (1,) * (array.ndim - 1 - axis_at))

    near = jax.random.permutation(own_key, blocks)[block_of(target)]
    other_side = (block_of(target) + blocks // 2) % blocks
    return jnp.where((block_of(source) == near) | (block_of(source) == other_side), factor * array, array)


def block_scale(rng, extent, pieces, low, largest):
    gain, own = 1.0, jax.random.fold_in(rng, 6)
    for axis_at, parts in pieces:
        heights = jnp.exp(jax.random.uniform(jax.random.fold_in(own, axis_at), (parts,), jnp.float32, low / len(pieces), largest / len(pieces)))
        gain = gain * jnp.repeat(heights, extent[axis_at] // parts).reshape([-1 if axis == axis_at else 1 for axis in range(len(extent))])
    return gain


def cumulative_ranks(count, slope):
    loads = [(1 << 20) // math.isqrt(standing ** slope) + 1 for standing in range(1, count + 1)]
    spread = 1 + sum(loads) // (1 << 30)
    return np.cumsum(np.array([max(1, weight // spread) for weight in loads]))


def skewed_ids(stream_key, dims, count, skew):
    grid = cumulative_ranks(count, skew)
    pick = jax.random.randint(jax.random.fold_in(stream_key, 1), dims, 0, int(grid[count - 1]))
    standing = jnp.searchsorted(jnp.asarray(grid, jnp.int32), pick, side="right")
    return jax.random.permutation(jax.random.fold_in(stream_key, 2), count)[standing].astype(jnp.int32)


def bell_draw(own_key, shape, scale, bound, cuts=(), held_as=jnp.bfloat16):
    result = scale * jax.random.normal(own_key, shape, jnp.float32)
    if cuts:
        result = result * block_scale(own_key, shape, cuts, -0.22, 0.18)
    return jnp.clip(result, -bound, bound).astype(held_as)


def bell_draw_with(key, extent, deviation, limit, pieces, heavy, kind=jnp.bfloat16):
    values = deviation * jax.random.normal(key, extent, jnp.float32)
    if pieces:
        values = values * block_scale(key, extent, pieces, -0.22, 0.18)
    return jnp.clip(spiked(values, jax.random.fold_in(key, 3), *heavy), -limit, limit).astype(kind)


def setup_inputs(seed: int = 0) -> dict:
    arg_keys = jax.random.split(jax.random.key(seed), 7)
    features = bell_draw_with(arg_keys[0], (BATCH, F), 1.0, 6.0, ((0, 32),), (0, 1, 32, 2.75))
    head_weight = bell_draw(arg_keys[1], (F, D), (F * D) ** -0.5, 0.0048828125)
    labels = plant(skewed_ids(arg_keys[2], (BATCH,), CLASSES, 3), jax.random.fold_in(arg_keys[2], 3), 0, CLASSES - 1).astype(jnp.int32)
    pos_index = plant(jax.random.randint(arg_keys[3], (BATCH, POSITIVES), 0, TILE), jax.random.fold_in(arg_keys[3], 1), 0, TILE - 1).astype(jnp.int32)
    pair_mask = draw_pair_mask(jax.random.fold_in(arg_keys[6], 71), 0)
    loss_weight = jnp.clip(jnp.exp(math.log(1.0) - 1.3862944 * jax.random.uniform(arg_keys[5], (BATCH,), jnp.float32) ** block_scale(arg_keys[5], (BATCH,), ((0, 32),), -0.2, 0.2)), 0.25, 1.0)
    return {"features": features, "head_weight": head_weight, "labels": labels, "pos_index": pos_index, "pair_mask": pair_mask, "loss_weight": loss_weight}


SMOOTHING_SCALE = 16.0
SLACK_GAP = 0.1


def score_tile(anchors, anchor_sq, anchor_labels, matching_separation, weights, tile_rows, tile_labels, listed):
    matching_samples = matching_separation.shape[1]
    block_tally = tile_rows.shape[0]
    anchor_count = anchors.shape[0]

    def compute(unused):
        products = lax.dot_general(anchors, tile_rows, (((1,), (1,)), ((), ())), preferred_element_type=jnp.float32)
        widened = tile_rows.astype(jnp.float32)
        tile_sq = jnp.sum(widened * widened, axis=1)
        couple_separation = anchor_sq[:, None] + tile_sq[None, :] - 2.0 * products
        valid = (anchor_labels[:, None] != tile_labels[None, :]).astype(jnp.float32)
        weighting = weights / (matching_samples * block_tally)
        objective_accrued = jnp.zeros((anchor_count,), jnp.float32)
        coefficient = jnp.zeros((anchor_count, block_tally), jnp.float32)
        totals = []
        for target_slot in range(matching_samples):
            slack_excess = SMOOTHING_SCALE * (matching_separation[:, target_slot:target_slot + 1] - couple_separation + SLACK_GAP)
            objective_accrued = objective_accrued + jnp.sum(valid * jax.nn.softplus(slack_excess), axis=1)
            sigmoids = valid * jax.nn.sigmoid(slack_excess)
            coefficient = coefficient + sigmoids
            totals.append(jnp.sum(sigmoids, axis=1))
        objective_accrued = objective_accrued / (SMOOTHING_SCALE * matching_samples * block_tally)
        coefficient = coefficient * weighting[:, None]
        pos_coef = jnp.stack(totals, axis=1) * weighting[:, None]
        coef_low = coefficient.astype(jnp.bfloat16)
        anchor_grad = 2.0 * jnp.dot(coef_low, tile_rows, preferred_element_type=jnp.float32)
        pulled = lax.dot_general(coef_low, anchors, (((0,), (0,)), ((), ())), preferred_element_type=jnp.float32)
        tile_grad = 2.0 * (pulled - jnp.sum(coefficient, axis=0)[:, None] * widened)
        return objective_accrued, pos_coef, anchor_grad, tile_grad

    def skip(unused):
        return (jnp.zeros((anchor_count,), jnp.float32),
                jnp.zeros((anchor_count, matching_samples), jnp.float32),
                jnp.zeros((anchor_count, anchors.shape[1]), jnp.float32),
                jnp.zeros((block_tally, anchors.shape[1]), jnp.float32))

    return lax.cond(listed, compute, skip, 0)


def reference(features, head_weight, labels, pos_index, pair_mask, loss_weight):
    embedded = jnp.dot(features, head_weight, preferred_element_type=jnp.float32).astype(jnp.bfloat16)
    widened = embedded.astype(jnp.float32)
    squares = jnp.sum(widened * widened, axis=1)
    tile_emb = embedded.reshape(N_BLK, TILE, D)
    tile_sq = squares.reshape(N_BLK, TILE)
    tile_lab = labels.reshape(N_BLK, TILE)
    tile_pos = pos_index.reshape(N_BLK, TILE, POSITIVES)
    tile_weight = loss_weight.reshape(N_BLK, TILE)

    def per_tile(term_total, inputs):
        index, anchors, anchor_sq, anchor_labels, positions, weights, mask_row = inputs
        pos_rows = anchors[positions]
        pos_wide = pos_rows.astype(jnp.float32)
        pos_sq = anchor_sq[positions]
        matching_separation = anchor_sq[:, None] + pos_sq - 2.0 * jnp.einsum(
            "ad,akd->ak", anchors.astype(jnp.float32), pos_wide)
        loss_total = jnp.zeros((TILE,), jnp.float32)
        coef_total = jnp.zeros((TILE, POSITIVES), jnp.float32)
        grad_total = jnp.zeros((TILE, D), jnp.float32)
        for offset in range(BAND):
            target = (index - offset) % N_BLK
            tile_rows = lax.dynamic_index_in_dim(tile_emb, target, 0, keepdims=False)
            tile_labels = lax.dynamic_index_in_dim(tile_lab, target, 0, keepdims=False)
            loss_part, coef_part, grad_part, term_part = score_tile(
                anchors, anchor_sq, anchor_labels, matching_separation, weights, tile_rows, tile_labels, mask_row[offset] > 0)
            loss_total = loss_total + loss_part
            coef_total = coef_total + coef_part
            grad_total = grad_total + grad_part
            current = lax.dynamic_index_in_dim(term_total, target, 0, keepdims=False)
            term_total = lax.dynamic_update_index_in_dim(term_total, current + term_part, target, 0)
        grad_total = grad_total - 2.0 * jnp.sum(coef_total[:, :, None] * pos_wide, axis=1)
        pushed = 2.0 * coef_total[:, :, None] * (pos_wide - anchors.astype(jnp.float32)[:, None, :])
        own_term = jnp.zeros((TILE, D), jnp.float32).at[positions.reshape(-1)].add(pushed.reshape(-1, D))
        current = lax.dynamic_index_in_dim(term_total, index, 0, keepdims=False)
        term_total = lax.dynamic_update_index_in_dim(term_total, current + own_term, index, 0)
        return term_total, (loss_total, grad_total)

    start_terms = jnp.zeros((N_BLK, TILE, D), jnp.float32)
    term_total, outputs = lax.scan(per_tile, start_terms, (jnp.arange(N_BLK, dtype=jnp.int32), tile_emb, tile_sq, tile_lab, tile_pos, tile_weight, pair_mask))
    loss_tiles, grad_tiles = outputs
    emb_grad = grad_tiles.reshape(BATCH, D) + term_total.reshape(BATCH, D)
    grad_low = emb_grad.astype(jnp.bfloat16)
    weight_grad = jnp.dot(features.T, grad_low, preferred_element_type=jnp.float32)
    return loss_tiles.reshape(BATCH), weight_grad
```

```python
import functools

import jax
import jax.numpy as jnp
from jax import lax
from jax.experimental import pallas as pl
from jax.experimental.pallas import tpu as pltpu
from jax.sharding import PartitionSpec as P

SMOOTHING_SCALE = 16.0
SLACK_GAP = 0.1


def passed_along(block, axis, distance):
    devices = range(lax.axis_size(axis))
    route = [((i - distance) % len(devices), i) for i in devices]
    return lax.ppermute(block, axis, route)


def score_tile(
    anchors, anchor_sq, anchor_labels, matching_separation, weights, tile_rows, tile_labels, listed
):
    matching_samples = matching_separation.shape[1]
    block_tally = tile_rows.shape[0]
    anchor_count = anchors.shape[0]

    def compute(unused):
        products = lax.dot_general(
            anchors, tile_rows, (((1,), (1,)), ((), ())), preferred_element_type=jnp.float32
        )
        widened = tile_rows.astype(jnp.float32)
        tile_sq = jnp.sum(widened * widened, axis=1)
        couple_separation = anchor_sq[:, None] + tile_sq[None, :] - 2.0 * products
        valid = (anchor_labels[:, None] != tile_labels[None, :]).astype(jnp.float32)
        weighting = weights / (matching_samples * block_tally)
        objective_accrued = jnp.zeros((anchor_count,), jnp.float32)
        coefficient = jnp.zeros((anchor_count, block_tally), jnp.float32)
        totals = []
        for target_slot in range(matching_samples):
            slack_excess = SMOOTHING_SCALE * (
                matching_separation[:, target_slot : target_slot + 1]
                - couple_separation
                + SLACK_GAP
            )
            objective_accrued = objective_accrued + jnp.sum(
                valid * jax.nn.softplus(slack_excess), axis=1
            )
            sigmoids = valid * jax.nn.sigmoid(slack_excess)
            coefficient = coefficient + sigmoids
            totals.append(jnp.sum(sigmoids, axis=1))
        objective_accrued = objective_accrued / (SMOOTHING_SCALE * matching_samples * block_tally)
        coefficient = coefficient * weighting[:, None]
        pos_coef = jnp.stack(totals, axis=1) * weighting[:, None]
        coef_low = coefficient.astype(jnp.bfloat16)
        anchor_grad = 2.0 * jnp.dot(coef_low, tile_rows, preferred_element_type=jnp.float32)
        pulled = lax.dot_general(
            coef_low, anchors, (((0,), (0,)), ((), ())), preferred_element_type=jnp.float32
        )
        col_sums = jnp.sum(coefficient, axis=0)
        tile_grad = 2.0 * (pulled - col_sums[:, None] * widened)
        return (objective_accrued, pos_coef, anchor_grad, tile_grad, coef_low, col_sums)

    def skip(unused):
        return (
            jnp.zeros((anchor_count,), jnp.float32),
            jnp.zeros((anchor_count, matching_samples), jnp.float32),
            jnp.zeros((anchor_count, anchors.shape[1]), jnp.float32),
            jnp.zeros((block_tally, anchors.shape[1]), jnp.float32),
            jnp.zeros((anchor_count, block_tally), jnp.bfloat16),
            jnp.zeros((block_tally,), jnp.float32),
        )

    return lax.cond(listed, compute, skip, 0)


def local(features, head_weight, labels, pos_index, pair_mask, loss_weight):
    embedded = jnp.dot(features, head_weight, preferred_element_type=jnp.float32).astype(
        jnp.bfloat16
    )
    widened = embedded.astype(jnp.float32)
    anchor_sq = jnp.sum(widened * widened, axis=1)
    tile_rows, tile_labels = (
        lax.all_gather(embedded, "rows", axis=0, tiled=True),
        lax.all_gather(labels, "rows", axis=0, tiled=True),
    )
    pos_rows = tile_rows[pos_index]
    pos_wide = pos_rows.astype(jnp.float32)
    pos_sq = jnp.sum(pos_wide * pos_wide, axis=2)
    matching_separation = (
        anchor_sq[:, None]
        + pos_sq
        - 2.0 * jnp.einsum("ad,akd->ak", embedded, pos_rows, preferred_element_type=jnp.float32)
    )
    offsets = pair_mask.shape[1]
    loss_total, coef_total, grad_total, own_term, first_low, first_sums = score_tile(
        embedded,
        anchor_sq,
        labels,
        matching_separation,
        loss_weight,
        tile_rows,
        tile_labels,
        pair_mask[0, 0] > 0,
    )
    received = jnp.zeros_like(own_term)
    walk_rows, walk_labels = (tile_rows, tile_labels)
    for offset in range(1, offsets):
        walk_rows, walk_labels = passed_along((walk_rows, walk_labels), "blk", 1)
        loss_part, coef_part, grad_part, term_part, low_part, sums_part = score_tile(
            embedded,
            anchor_sq,
            labels,
            matching_separation,
            loss_weight,
            walk_rows,
            walk_labels,
            pair_mask[0, offset] > 0,
        )
        loss_total = loss_total + loss_part
        coef_total = coef_total + coef_part
        grad_total = grad_total + grad_part
        received = received + passed_along(term_part.astype(jnp.bfloat16), "blk", -offset).astype(
            term_part.dtype
        )
    grad_total = grad_total - 2.0 * jnp.sum(coef_total[:, :, None] * pos_wide, axis=1)
    pushed = 2.0 * coef_total[:, :, None] * (pos_wide - widened[:, None, :])
    own_term = own_term.at[pos_index.reshape(-1)].add(pushed.reshape(-1, pushed.shape[2]))
    quarter_sum = lax.psum_scatter(own_term + received, "rows", scatter_dimension=0, tiled=True)
    emb_grad = grad_total + quarter_sum
    grad_low = emb_grad.astype(jnp.bfloat16)
    weight_grad = lax.psum_scatter(
        lax.dot_general(
            features, grad_low, (((0,), (0,)), ((), ())), preferred_element_type=jnp.float32
        ),
        ("blk", "rows"),
        scatter_dimension=0,
        tiled=True,
    )
    return (loss_total, weight_grad)


MESH = pl.DeviceIdType.MESH
NT = (((1,), (1,)), ((), ()))
TN = (((0,), (0,)), ((), ()))


def dot(a, b, dims=(((1,), (0,)), ((), ()))):
    return lax.dot_general(a, b, dims, preferred_element_type=jnp.float32)


def as_column(row):
    return jnp.transpose(jnp.broadcast_to(row, (128, row.shape[1])))[:, 0:1]


def kernel(
    f_ref, w_ref, meta_in, mask_ref, loss_ref, out_ref,
    ea, en, meta, metan, fc, acc, pul, cs, dpr, sqc, st, strec, tst, trec, ast, arec, ga, pst, prec,
    ea_s, ea_r, ma_s, ma_r, en_s, en_r, mn_s, mn_r, fc_s, fc_r, t_s, t_r, a_s, a_r,
    st_s, st_r, g_s, g_r, p_s, p_r,
):
    nb = lax.axis_size("blk")
    t = lax.axis_index("blk")
    r = lax.axis_index("rows")
    y, c = r // 2, r % 2
    mate = 2 * y + 1 - c
    across = 2 * (1 - y) + c
    diag = 2 * (1 - y) + 1 - c
    peers = (mate, across, diag)
    quarter, width = f_ref.shape[0], w_ref.shape[1]
    tile = 4 * quarter

    def push(src, dst, ss, rs, dev):
        copy = pltpu.make_async_remote_copy(
            src_ref=src, dst_ref=dst, send_sem=ss, recv_sem=rs, device_id=dev, device_id_type=MESH
        )
        copy.start()
        return copy

    def landed(dst, ss, rs):
        pltpu.make_async_remote_copy(
            src_ref=dst, dst_ref=dst, send_sem=ss, recv_sem=rs, device_id=(t, mate), device_id_type=MESH
        ).wait_recv()

    barrier = pltpu.get_barrier_semaphore()
    for step in range(nb):
        for core in range(2):
            if step == 0 and core == 0:
                continue
            dev = ((t + step) % nb, 2 * y + (c + core) % 2)
            pl.semaphore_signal(barrier, inc=1, device_id=dev, device_id_type=MESH)
    for peer in (across, diag):
        pl.semaphore_signal(barrier, inc=1, device_id=(t, peer), device_id_type=MESH)

    square = jnp.zeros((quarter, 1), jnp.float32)
    for j in range(width // 256):
        part = dot(f_ref[...], w_ref[:, j * 256 : (j + 1) * 256]).astype(jnp.bfloat16)
        ea[r, :, j * 256 : (j + 1) * 256] = part
        wide = part.astype(jnp.float32)
        square = square + jnp.sum(wide * wide, axis=1, keepdims=True)
    meta[r] = meta_in[...]
    meta[r, 5:6, :] = jnp.transpose(jnp.broadcast_to(square, (quarter, 128)))[0:1, :]
    pl.semaphore_wait(barrier, 2 * nb + 1)

    sent = []
    for n, peer in ((1, across), (0, mate)):
        sent.append(push(ea.at[r], ea.at[r], ea_s.at[n], ea_r.at[r], (t, peer)))
        sent.append(push(meta.at[r], meta.at[r], ma_s.at[n], ma_r.at[r], (t, peer)))
    for s in (2, 1):
        dev = ((t + s) % nb, r)
        sent.append(push(ea.at[r], en.at[s - 1], en_s.at[s - 1], en_r.at[s - 1], dev))
        sent.append(push(meta.at[r], metan.at[s - 1], mn_s.at[s - 1], mn_r.at[s - 1], dev))
    landed(ea.at[across], ea_s.at[0], ea_r.at[across])
    sent.append(push(ea.at[across], ea.at[across], ea_s.at[2], ea_r.at[across], (t, mate)))
    landed(meta.at[across], ma_s.at[0], ma_r.at[across])
    sent.append(push(meta.at[across], meta.at[across], ma_s.at[2], ma_r.at[across], (t, mate)))
    for n, peer in enumerate(peers):
        for i in range(4):
            column = ((2 * (4 * (peer % 2) + i)) + peer // 2) * 128
            sent.append(
                push(
                    f_ref.at[:, pl.ds(pl.multiple_of(column, 128), 128)],
                    fc.at[r, i], fc_s.at[n, i], fc_r.at[r, i], (t, peer),
                )
            )
    for i in range(4):
        column = ((2 * (4 * c + i)) + y) * 128
        fc[r, i] = f_ref[:, pl.ds(pl.multiple_of(column, 128), 128)]
    for peer in (mate, diag):
        landed(ea.at[peer], ea_s.at[0], ea_r.at[peer])
        landed(meta.at[peer], ma_s.at[0], ma_r.at[peer])

    sub = lax.broadcasted_iota(jnp.int32, (quarter, quarter), 0)
    subf = sub.astype(jnp.float32)
    for n in range(4):
        sqc[n] = jnp.broadcast_to(as_column(meta[n, 5:6, :]), (quarter, 128))

    def positives(a, carry):
        anchors = ea[a]
        found = [jnp.zeros((1, quarter), jnp.float32) for _ in range(3)]
        for n in range(4):
            d = sqc[n][:, 0:1] - 2.0 * dot(ea[n], anchors, NT)
            for k in range(3):
                hit = meta[a, 1 + k : 2 + k, :] == subf + float(n * quarter)
                found[k] = found[k] + jnp.sum(jnp.where(hit, d, 0.0), axis=0, keepdims=True)
        for k in range(3):
            dpr[a, k : k + 1, :] = found[k] + meta[a, 5:6, :]
        st[a] = jnp.zeros((8, quarter), jnp.float32)
        acc[a] = jnp.zeros((quarter, width), jnp.float32)
        return carry

    lax.fori_loop(0, 4, positives, 0)

    def score(s, rows, lab_row, sq_row):
        lab_n = as_column(lab_row)
        sq_n = as_column(sq_row)
        pul[...] = jnp.zeros((quarter, width), jnp.float32)
        cs[...] = jnp.zeros((quarter, 128), jnp.float32)

        def chunk(a, carry):
            anchors = ea[a]
            dist = (meta[a, 5:6, :] + sq_n) - 2.0 * dot(rows(), anchors, NT)
            valid = jnp.where(lab_n != meta[a, 0:1, :], mask_ref[s : s + 1, :], 0.0)
            coef = jnp.zeros((quarter, quarter), jnp.float32)
            loss = jnp.zeros((quarter, quarter), jnp.float32)
            for k in range(3):
                x = SMOOTHING_SCALE * (dpr[a, k : k + 1, :] - dist + SLACK_GAP)
                e = jnp.exp(-jnp.abs(x))
                loss = loss + (jnp.maximum(x, 0.0) + jnp.log1p(e))
                inv = 1.0 / (1.0 + e)
                sig = valid * jnp.where(x >= 0, inv, e * inv)
                coef = coef + sig
                st[a, 1 + k : 2 + k, :] += jnp.sum(sig, axis=0, keepdims=True)
            st[a, 0:1, :] += jnp.sum(valid * loss, axis=0, keepdims=True)
            coef = coef * (meta[a, 4:5, :] / (3.0 * tile))
            low = coef.astype(jnp.bfloat16)
            cs[...] += jnp.broadcast_to(jnp.sum(coef, axis=1, keepdims=True), (quarter, 128))
            pul[...] += dot(low, anchors)
            acc[a] += dot(low, rows(), TN)
            return carry

        lax.fori_loop(0, 4, chunk, 0)
        return 2.0 * (pul[...] - cs[:, 0:1] * rows().astype(jnp.float32))

    for s in (1, 2):
        landed(en.at[s - 1], en_s.at[s - 1], en_r.at[s - 1])
        landed(metan.at[s - 1], mn_s.at[s - 1], mn_r.at[s - 1])
        term = score(s, lambda: en[s - 1], metan[s - 1, 0:1, :], metan[s - 1, 5:6, :])
        tst[s - 1] = term.astype(jnp.bfloat16)
        sent.append(
            push(tst.at[s - 1], trec.at[s - 1], t_s.at[s - 1], t_r.at[s - 1], ((t + nb - s) % nb, r))
        )
    own = score(0, lambda: ea[r], meta[r, 0:1, :], meta[r, 5:6, :])
    pul[...] = own
    for n, peer in enumerate(peers):
        sent.append(push(st, strec.at[r], st_s.at[n], st_r.at[r], (t, peer)))
    for n, peer in ((1, across), (2, diag), (0, mate)):
        ast[n] = (2.0 * acc[peer]).astype(jnp.bfloat16)
        sent.append(push(ast.at[n], arec.at[r], a_s.at[n], a_r.at[r], (t, peer)))

    strec[r] = st[...]
    for peer in peers:
        landed(strec.at[peer], st_s.at[0], st_r.at[peer])
    for a in range(4):
        dpr[a] = strec[0, a] + strec[1, a] + strec[2, a] + strec[3, a]
    loss_ref[...] = dpr[r] * (1.0 / (SMOOTHING_SCALE * 3.0 * tile))

    acc[r] = 2.0 * acc[r] + pul[...]
    cs[...] = jnp.zeros((quarter, 128), jnp.float32)

    def listed(a, first):
        wgt = meta[a, 4:5, :] * (1.0 / (3.0 * tile))
        out = jnp.zeros((quarter, quarter), jnp.float32)
        for k in range(3):
            hit = meta[a, 1 + k : 2 + k, :] == subf + first
            out = out + jnp.where(hit, dpr[a, 1 + k : 2 + k, :] * wgt, 0.0)
        high = out.astype(jnp.bfloat16)
        return out, high, (out - high.astype(jnp.float32)).astype(jnp.bfloat16)

    def pulls(n, carry):
        out, high, low = listed(n, (r * quarter).astype(jnp.float32))
        cs[...] += jnp.broadcast_to(jnp.sum(out, axis=1, keepdims=True), (quarter, 128))
        pushed = dot(high, ea[n]) + dot(low, ea[n])
        out, high, low = listed(r, (n * quarter).astype(jnp.float32))
        drawn = dot(high, ea[n], TN) + dot(low, ea[n], TN)
        acc[r] -= 2.0 * (pushed + drawn)
        return carry

    lax.fori_loop(0, 4, pulls, 0)
    total = acc[r] + 2.0 * cs[:, 0:1] * ea[r].astype(jnp.float32)
    for peer in peers:
        landed(arec.at[peer], a_s.at[0], a_r.at[peer])
        total = total + arec[peer].astype(jnp.float32)
    for s in (1, 2):
        landed(trec.at[s - 1], t_s.at[s - 1], t_r.at[s - 1])
        total = total + trec[s - 1].astype(jnp.float32)
    ga[r] = total.astype(jnp.bfloat16)
    for n, peer in ((1, across), (0, mate)):
        sent.append(push(ga.at[r], ga.at[r], g_s.at[n], g_r.at[r], (t, peer)))
    landed(ga.at[across], g_s.at[0], g_r.at[across])
    sent.append(push(ga.at[across], ga.at[across], g_s.at[2], g_r.at[across], (t, mate)))
    for peer in peers:
        for i in range(4):
            landed(fc.at[peer, i], fc_s.at[0, i], fc_r.at[peer, i])
    for peer in (mate, diag):
        landed(ga.at[peer], g_s.at[0], g_r.at[peer])

    half = out_ref.shape[0]

    def away(i, h):
        return jnp.logical_or(4 * c + i != t, c != h)

    for i in range(4):
        part = dot(fc[0, i], ga[0], TN)
        for n in range(1, 4):
            part = part + dot(fc[n, i], ga[n], TN)
        part = part.astype(jnp.bfloat16)
        for h in range(2):
            pst[i, h] = part[h * half : (h + 1) * half]
        for h in range(2):
            @pl.when(away(i, h))
            def _():
                push(pst.at[i, h], prec.at[t], p_s.at[i, h], p_r.at[t], (4 * c + i, 2 * y + h))

            @pl.when(jnp.logical_not(away(i, h)))
            def _():
                prec[t] = pst[i, h]

    for step in range(nb):
        @pl.when(jnp.logical_or(t // 4 != c, t != step))
        def _():
            landed(prec.at[step], p_s.at[0, 0], p_r.at[step])

    result = prec[0].astype(jnp.float32)
    for step in range(1, nb):
        result = result + prec[step].astype(jnp.float32)
    out_ref[...] = result
    for i in range(4):
        for h in range(2):
            @pl.when(away(i, h))
            def _():
                pltpu.make_async_remote_copy(
                    src_ref=pst.at[i, h], dst_ref=prec.at[t], send_sem=p_s.at[i, h],
                    recv_sem=p_r.at[t], device_id=(t, mate), device_id_type=MESH,
                ).wait_send()
    for copy in sent:
        copy.wait_send()


def fused(features, head_weight, labels, pos_index, pair_mask, loss_weight):
    quarter, depth = features.shape
    width = head_weight.shape[1]
    nb = lax.axis_size("blk")
    share = depth // (4 * nb)
    meta = jnp.concatenate(
        [
            labels.astype(jnp.float32)[None, :],
            pos_index.astype(jnp.float32).T,
            loss_weight[None, :],
            jnp.zeros((3, quarter), jnp.float32),
        ]
    )
    mask = jnp.zeros((8, quarter), jnp.float32).at[:3].set(
        jnp.broadcast_to((pair_mask[0] > 0).astype(jnp.float32)[:, None], (3, quarter))
    )
    f32, bf16 = jnp.float32, jnp.bfloat16
    dma = pltpu.SemaphoreType.DMA
    vmem = pl.BlockSpec(memory_space=pltpu.VMEM)
    block = (quarter, width)
    small = (8, quarter)
    loss, grad = pl.pallas_call(
        kernel,
        out_shape=(jax.ShapeDtypeStruct(small, f32), jax.ShapeDtypeStruct((share, width), f32)),
        in_specs=[vmem] * 4,
        out_specs=(vmem, vmem),
        scratch_shapes=[
            pltpu.VMEM((4,) + block, bf16),
            pltpu.VMEM((2,) + block, bf16),
            pltpu.VMEM((4,) + small, f32),
            pltpu.VMEM((2,) + small, f32),
            pltpu.VMEM((4, 4, quarter, 128), bf16),
            pltpu.VMEM((4,) + block, f32),
            pltpu.VMEM(block, f32),
            pltpu.VMEM((quarter, 128), f32),
            pltpu.VMEM((4,) + small, f32),
            pltpu.VMEM((4, quarter, 128), f32),
            pltpu.VMEM((4,) + small, f32),
            pltpu.VMEM((4, 4) + small, f32),
            pltpu.VMEM((2,) + block, bf16),
            pltpu.VMEM((2,) + block, bf16),
            pltpu.VMEM((3,) + block, bf16),
            pltpu.VMEM((4,) + block, bf16),
            pltpu.VMEM((4,) + block, bf16),
            pltpu.VMEM((4, 2, share, width), bf16),
            pltpu.VMEM((nb, share, width), bf16),
            dma((3,)), dma((4,)), dma((3,)), dma((4,)),
            dma((2,)), dma((2,)), dma((2,)), dma((2,)),
            dma((3, 4)), dma((4, 4)), dma((2,)), dma((2,)), dma((3,)), dma((4,)),
            dma((3,)), dma((4,)), dma((3,)), dma((4,)), dma((4, 2)), dma((nb,)),
        ],
        compiler_params=pltpu.CompilerParams(
            collective_id=0, has_side_effects=True, vmem_limit_bytes=56 * 1024 * 1024
        ),
    )(features, head_weight, meta, mask)
    return loss[0], grad


def solution(mesh):
    body = fused if mesh.shape["blk"] == 8 and mesh.shape["rows"] == 4 else local
    return jax.shard_map(
        body,
        mesh=mesh,
        in_specs=(
            P(("blk", "rows"), None),
            P(),
            P(("blk", "rows")),
            P(("blk", "rows"), None),
            P("blk", None),
            P(("blk", "rows")),
        ),
        out_specs=(P(("blk", "rows")), P(("blk", "rows"), None)),
        check_vma=False,
    )
```

```python
import functools

import jax
import jax.numpy as jnp
from jax import lax
from jax.experimental import pallas as pl
from jax.experimental.pallas import tpu as pltpu
from jax.sharding import PartitionSpec as P

SMOOTHING_SCALE = 16.0
SLACK_GAP = 0.1


def passed_along(block, axis, distance):
    devices = range(lax.axis_size(axis))
    route = [((i - distance) % len(devices), i) for i in devices]
    return lax.ppermute(block, axis, route)


def score_tile(
    anchors, anchor_sq, anchor_labels, matching_separation, weights, tile_rows, tile_labels, listed
):
    matching_samples = matching_separation.shape[1]
    block_tally = tile_rows.shape[0]
    anchor_count = anchors.shape[0]

    def compute(unused):
        products = lax.dot_general(
            anchors, tile_rows, (((1,), (1,)), ((), ())), preferred_element_type=jnp.float32
        )
        widened = tile_rows.astype(jnp.float32)
        tile_sq = jnp.sum(widened * widened, axis=1)
        couple_separation = anchor_sq[:, None] + tile_sq[None, :] - 2.0 * products
        valid = (anchor_labels[:, None] != tile_labels[None, :]).astype(jnp.float32)
        weighting = weights / (matching_samples * block_tally)
        objective_accrued = jnp.zeros((anchor_count,), jnp.float32)
        coefficient = jnp.zeros((anchor_count, block_tally), jnp.float32)
        totals = []
        for target_slot in range(matching_samples):
            slack_excess = SMOOTHING_SCALE * (
                matching_separation[:, target_slot : target_slot + 1]
                - couple_separation
                + SLACK_GAP
            )
            objective_accrued = objective_accrued + jnp.sum(
                valid * jax.nn.softplus(slack_excess), axis=1
            )
            sigmoids = valid * jax.nn.sigmoid(slack_excess)
            coefficient = coefficient + sigmoids
            totals.append(jnp.sum(sigmoids, axis=1))
        objective_accrued = objective_accrued / (SMOOTHING_SCALE * matching_samples * block_tally)
        coefficient = coefficient * weighting[:, None]
        pos_coef = jnp.stack(totals, axis=1) * weighting[:, None]
        coef_low = coefficient.astype(jnp.bfloat16)
        anchor_grad = 2.0 * jnp.dot(coef_low, tile_rows, preferred_element_type=jnp.float32)
        pulled = lax.dot_general(
            coef_low, anchors, (((0,), (0,)), ((), ())), preferred_element_type=jnp.float32
        )
        col_sums = jnp.sum(coefficient, axis=0)
        tile_grad = 2.0 * (pulled - col_sums[:, None] * widened)
        return (objective_accrued, pos_coef, anchor_grad, tile_grad, coef_low, col_sums)

    def skip(unused):
        return (
            jnp.zeros((anchor_count,), jnp.float32),
            jnp.zeros((anchor_count, matching_samples), jnp.float32),
            jnp.zeros((anchor_count, anchors.shape[1]), jnp.float32),
            jnp.zeros((block_tally, anchors.shape[1]), jnp.float32),
            jnp.zeros((anchor_count, block_tally), jnp.bfloat16),
            jnp.zeros((block_tally,), jnp.float32),
        )

    return lax.cond(listed, compute, skip, 0)


def local(features, head_weight, labels, pos_index, pair_mask, loss_weight):
    embedded = jnp.dot(features, head_weight, preferred_element_type=jnp.float32).astype(
        jnp.bfloat16
    )
    widened = embedded.astype(jnp.float32)
    anchor_sq = jnp.sum(widened * widened, axis=1)
    tile_rows, tile_labels = (
        lax.all_gather(embedded, "rows", axis=0, tiled=True),
        lax.all_gather(labels, "rows", axis=0, tiled=True),
    )
    pos_rows = tile_rows[pos_index]
    pos_wide = pos_rows.astype(jnp.float32)
    pos_sq = jnp.sum(pos_wide * pos_wide, axis=2)
    matching_separation = (
        anchor_sq[:, None]
        + pos_sq
        - 2.0 * jnp.einsum("ad,akd->ak", embedded, pos_rows, preferred_element_type=jnp.float32)
    )
    offsets = pair_mask.shape[1]
    loss_total, coef_total, grad_total, own_term, first_low, first_sums = score_tile(
        embedded,
        anchor_sq,
        labels,
        matching_separation,
        loss_weight,
        tile_rows,
        tile_labels,
        pair_mask[0, 0] > 0,
    )
    received = jnp.zeros_like(own_term)
    walk_rows, walk_labels = (tile_rows, tile_labels)
    for offset in range(1, offsets):
        walk_rows, walk_labels = passed_along((walk_rows, walk_labels), "blk", 1)
        loss_part, coef_part, grad_part, term_part, low_part, sums_part = score_tile(
            embedded,
            anchor_sq,
            labels,
            matching_separation,
            loss_weight,
            walk_rows,
            walk_labels,
            pair_mask[0, offset] > 0,
        )
        loss_total = loss_total + loss_part
        coef_total = coef_total + coef_part
        grad_total = grad_total + grad_part
        received = received + passed_along(term_part.astype(jnp.bfloat16), "blk", -offset).astype(
            term_part.dtype
        )
    grad_total = grad_total - 2.0 * jnp.sum(coef_total[:, :, None] * pos_wide, axis=1)
    pushed = 2.0 * coef_total[:, :, None] * (pos_wide - widened[:, None, :])
    own_term = own_term.at[pos_index.reshape(-1)].add(pushed.reshape(-1, pushed.shape[2]))
    quarter_sum = lax.psum_scatter(own_term + received, "rows", scatter_dimension=0, tiled=True)
    emb_grad = grad_total + quarter_sum
    grad_low = emb_grad.astype(jnp.bfloat16)
    weight_grad = lax.psum_scatter(
        lax.dot_general(
            features, grad_low, (((0,), (0,)), ((), ())), preferred_element_type=jnp.float32
        ),
        ("blk", "rows"),
        scatter_dimension=0,
        tiled=True,
    )
    return (loss_total, weight_grad)


MESH = pl.DeviceIdType.MESH
NT = (((1,), (1,)), ((), ()))
TN = (((0,), (0,)), ((), ()))


def dot(a, b, dims=(((1,), (0,)), ((), ()))):
    return lax.dot_general(a, b, dims, preferred_element_type=jnp.float32)


def as_column(row):
    return jnp.transpose(jnp.broadcast_to(row, (128, row.shape[1])))[:, 0:1]


def kernel(
    f_ref, w_ref, lab_ref, pos_ref, wgt_ref, mask_ref, loss_ref, out_ref,
    ea, en, meta, metan, fc, fct, acc, own, pul, cs, dpr, sqc, st, strec, tst, trec, ast, arec, hst, hrec,
    ga, pst, prec,
    ea_s, ea_r, ma_s, ma_r, en_s, en_r, mn_s, mn_r, fc_s, fc_r, t_s, t_r, a_s, a_r,
    h_s, h_r, st_s, st_r, g_s, g_r, p_s, p_r,
):
    nb = lax.axis_size("blk")
    t = lax.axis_index("blk")
    r = lax.axis_index("rows")
    y, c = r // 2, r % 2
    mate = 2 * y + 1 - c
    across = 2 * (1 - y) + c
    diag = 2 * (1 - y) + 1 - c
    peers = (mate, across, diag)
    quarter, width = f_ref.shape[0], w_ref.shape[1]
    tile = 4 * quarter

    def push(src, dst, ss, rs, dev):
        copy = pltpu.make_async_remote_copy(
            src_ref=src, dst_ref=dst, send_sem=ss, recv_sem=rs, device_id=dev, device_id_type=MESH
        )
        copy.start()
        return copy

    def landed(dst, ss, rs):
        pltpu.make_async_remote_copy(
            src_ref=dst, dst_ref=dst, send_sem=ss, recv_sem=rs, device_id=(t, mate), device_id_type=MESH
        ).wait_recv()

    barrier = pltpu.get_barrier_semaphore()
    for step in range(nb):
        for core in range(2):
            if step == 0 and core == 0:
                continue
            dev = ((t + step) % nb, 2 * y + (c + core) % 2)
            pl.semaphore_signal(barrier, inc=1, device_id=dev, device_id_type=MESH)
    for peer in (across, diag):
        pl.semaphore_signal(barrier, inc=1, device_id=(t, peer), device_id_type=MESH)

    square = jnp.zeros((quarter, 1), jnp.float32)
    for j in range(width // 256):
        part = dot(f_ref[...], w_ref[:, j * 256 : (j + 1) * 256]).astype(jnp.bfloat16)
        ea[r, :, j * 256 : (j + 1) * 256] = part
        wide = part.astype(jnp.float32)
        square = square + jnp.sum(wide * wide, axis=1, keepdims=True)
    meta[r] = jnp.zeros(meta.shape[1:], jnp.float32)
    meta[r, 0:1, :] = lab_ref[...].astype(jnp.float32)
    meta[r, 1:4, :] = pos_ref[...].astype(jnp.float32)
    meta[r, 4:5, :] = wgt_ref[...]
    meta[r, 5:6, :] = jnp.transpose(jnp.broadcast_to(square, (quarter, 128)))[0:1, :]
    pl.semaphore_wait(barrier, 2 * nb + 1)

    sent = []
    for n, peer in ((1, across), (0, mate)):
        sent.append(push(ea.at[r], ea.at[r], ea_s.at[n], ea_r.at[r], (t, peer)))
        sent.append(push(meta.at[r], meta.at[r], ma_s.at[n], ma_r.at[r], (t, peer)))
    for s in (2, 1):
        dev = ((t + s) % nb, r)
        sent.append(push(ea.at[r], en.at[s - 1], en_s.at[s - 1], en_r.at[s - 1], dev))
        sent.append(push(meta.at[r], metan.at[s - 1], mn_s.at[s - 1], mn_r.at[s - 1], dev))
    landed(ea.at[across], ea_s.at[0], ea_r.at[across])
    sent.append(push(ea.at[across], ea.at[across], ea_s.at[2], ea_r.at[across], (t, mate)))
    landed(meta.at[across], ma_s.at[0], ma_r.at[across])
    sent.append(push(meta.at[across], meta.at[across], ma_s.at[2], ma_r.at[across], (t, mate)))
    for n, peer in enumerate(peers):
        for i in range(4):
            column = ((2 * (4 * (peer % 2) + i)) + peer // 2) * 128
            sent.append(
                push(
                    f_ref.at[:, pl.ds(pl.multiple_of(column, 128), 128)],
                    fc.at[r, i], fc_s.at[n, i], fc_r.at[r, i], (t, peer),
                )
            )
    for i in range(4):
        column = ((2 * (4 * c + i)) + y) * 128
        fc[r, i] = f_ref[:, pl.ds(pl.multiple_of(column, 128), 128)]
    for peer in (mate, diag):
        landed(ea.at[peer], ea_s.at[0], ea_r.at[peer])
        landed(meta.at[peer], ma_s.at[0], ma_r.at[peer])

    sub = lax.broadcasted_iota(jnp.int32, (quarter, quarter), 0)
    subf = sub.astype(jnp.float32)
    for n in range(4):
        sqc[n] = jnp.broadcast_to(as_column(meta[n, 5:6, :]), (quarter, 128))

    def positives(a, carry):
        anchors = ea[a]
        found = [jnp.zeros((1, quarter), jnp.float32) for _ in range(3)]
        for n in range(4):
            d = sqc[n][:, 0:1] - 2.0 * dot(ea[n], anchors, NT)
            for k in range(3):
                hit = meta[a, 1 + k : 2 + k, :] == subf + float(n * quarter)
                found[k] = found[k] + jnp.sum(jnp.where(hit, d, 0.0), axis=0, keepdims=True)
        for k in range(3):
            dpr[a, k : k + 1, :] = SMOOTHING_SCALE * (found[k] + meta[a, 5:6, :] + SLACK_GAP)
        st[a] = jnp.zeros((8, quarter), jnp.float32)
        acc[a] = jnp.zeros((quarter, width), jnp.float32)
        return carry

    lax.fori_loop(0, 4, positives, 0)

    def start_tile(lab_row, sq_row):
        pul[...] = jnp.zeros((quarter, width), jnp.float32)
        cs[...] = jnp.zeros((quarter, 128), jnp.float32)
        return as_column(lab_row), SMOOTHING_SCALE * as_column(sq_row)

    def chunk(s, a, rows, lab_n, sq_n):
        anchors = ea[a]
        spread = (SMOOTHING_SCALE * meta[a, 5:6, :] + sq_n) - (2.0 * SMOOTHING_SCALE) * dot(rows(), anchors, NT)
        scored = jnp.broadcast_to((mask_ref[0:1, s : s + 1] > 0).astype(jnp.float32), (1, quarter))
        valid = jnp.where(lab_n != meta[a, 0:1, :], scored, 0.0)
        linear = jnp.zeros((quarter, quarter), jnp.float32)
        e, top = [], []
        for k in range(3):
            x = dpr[a, k : k + 1, :] - spread
            e.append(jnp.exp(-jnp.abs(x)))
            top.append(jnp.where(x >= 0, 1.0, e[k]))
            linear = linear + jnp.maximum(x, 0.0)
        p = e[0] + e[1] + e[0] * e[1]
        p = p + e[2] + p * e[2]
        u = 1.0 + p
        inv = 1.0 / u
        log = jnp.log(u) + (p - (u - 1.0)) * inv
        st[a, 0:1, :] += jnp.sum(valid * (linear + log), axis=0, keepdims=True)
        inv = valid * inv
        coef = jnp.zeros((quarter, quarter), jnp.float32)
        for k in range(3):
            others = (1.0 + e[(k + 1) % 3]) * (1.0 + e[(k + 2) % 3])
            sig = top[k] * (inv * others)
            coef = coef + sig
            st[a, 1 + k : 2 + k, :] += jnp.sum(sig, axis=0, keepdims=True)
        coef = coef * (meta[a, 4:5, :] * (1.0 / (3.0 * tile)))
        low = coef.astype(jnp.bfloat16)
        cs[...] += jnp.broadcast_to(jnp.sum(coef, axis=1, keepdims=True), (quarter, 128))
        pul[...] += dot(low, anchors)
        acc[a] += dot(low, rows(), TN)

    def tile_term(rows):
        return 2.0 * (pul[...] - cs[:, 0:1] * rows().astype(jnp.float32))

    def score(s, rows, lab_row, sq_row):
        lab_n, sq_n = start_tile(lab_row, sq_row)

        def step(a, carry):
            chunk(s, a, rows, lab_n, sq_n)
            return carry

        lax.fori_loop(0, 4, step, 0)
        return tile_term(rows)

    def send_term(s, term):
        tst[s - 1] = term.astype(jnp.bfloat16)
        dev = ((t + nb - s) % nb, r)
        sent.append(push(tst.at[s - 1], trec.at[s - 1], t_s.at[s - 1], t_r.at[s - 1], dev))

    own[...] = score(0, lambda: ea[r], meta[r, 0:1, :], meta[r, 5:6, :])
    for s in (1, 2):
        landed(en.at[s - 1], en_s.at[s - 1], en_r.at[s - 1])
        landed(metan.at[s - 1], mn_s.at[s - 1], mn_r.at[s - 1])
    send_term(1, score(1, lambda: en[0], metan[0, 0:1, :], metan[0, 5:6, :]))

    lab_n, sq_n = start_tile(metan[1, 0:1, :], metan[1, 5:6, :])
    chunk(2, diag, lambda: en[1], lab_n, sq_n)
    hst[...] = (2.0 * acc[diag]).astype(jnp.bfloat16)
    sent.append(push(hst, hrec, h_s, h_r, (t, mate)))
    chunk(2, mate, lambda: en[1], lab_n, sq_n)
    ast[0] = (2.0 * acc[mate]).astype(jnp.bfloat16)
    sent.append(push(ast.at[0], arec.at[0], a_s.at[0], a_r.at[0], (t, mate)))
    chunk(2, across, lambda: en[1], lab_n, sq_n)
    landed(hrec, h_s, h_r)
    ast[1] = (2.0 * acc[across] + hrec[...].astype(jnp.float32)).astype(jnp.bfloat16)
    sent.append(push(ast.at[1], arec.at[1], a_s.at[1], a_r.at[1], (t, across)))
    chunk(2, r, lambda: en[1], lab_n, sq_n)
    for n, peer in enumerate(peers):
        sent.append(push(st, strec.at[r], st_s.at[n], st_r.at[r], (t, peer)))
    send_term(2, tile_term(lambda: en[1]))

    strec[r] = st[...]
    for peer in peers:
        landed(strec.at[peer], st_s.at[0], st_r.at[peer])
    for a in range(4):
        dpr[a] = strec[0, a] + strec[1, a] + strec[2, a] + strec[3, a]
    loss_ref[...] = dpr[r, 0:1, :] * (1.0 / (SMOOTHING_SCALE * 3.0 * tile))

    acc[r] = 2.0 * acc[r] + own[...]
    cs[...] = jnp.zeros((quarter, 128), jnp.float32)

    def listed(a, first):
        wgt = meta[a, 4:5, :] * (1.0 / (3.0 * tile))
        out = jnp.zeros((quarter, quarter), jnp.float32)
        for k in range(3):
            hit = meta[a, 1 + k : 2 + k, :] == subf + first
            out = out + jnp.where(hit, dpr[a, 1 + k : 2 + k, :] * wgt, 0.0)
        high = out.astype(jnp.bfloat16)
        return out, high, (out - high.astype(jnp.float32)).astype(jnp.bfloat16)

    def pulls(n, carry):
        out, high, low = listed(n, (r * quarter).astype(jnp.float32))
        cs[...] += jnp.broadcast_to(jnp.sum(out, axis=1, keepdims=True), (quarter, 128))
        pushed = dot(high, ea[n]) + dot(low, ea[n])
        out, high, low = listed(r, (n * quarter).astype(jnp.float32))
        drawn = dot(high, ea[n], TN) + dot(low, ea[n], TN)
        acc[r] -= 2.0 * (pushed + drawn)
        return carry

    lax.fori_loop(0, 4, pulls, 0)
    acc[r] += 2.0 * cs[:, 0:1] * ea[r].astype(jnp.float32)
    for peer in peers:
        for i in range(4):
            landed(fc.at[peer, i], fc_s.at[0, i], fc_r.at[peer, i])
    for n in range(4):
        for i in range(4):
            fct[i * 128 : (i + 1) * 128, n * quarter : (n + 1) * quarter] = jnp.transpose(fc[n, i])
    for n in range(2):
        landed(arec.at[n], a_s.at[0], a_r.at[n])
    for s in (1, 2):
        landed(trec.at[s - 1], t_s.at[s - 1], t_r.at[s - 1])
    pieces = ga.shape[0]
    piece = width // pieces
    for j in range(pieces):
        cut = slice(j * piece, (j + 1) * piece)
        total = acc[r, :, cut]
        for ref in (arec, trec):
            total = total + ref[0, :, cut].astype(jnp.float32) + ref[1, :, cut].astype(jnp.float32)
        ga[j, r] = total.astype(jnp.bfloat16)
        for n, peer in ((1, across), (0, mate)):
            sent.append(push(ga.at[j, r], ga.at[j, r], g_s.at[j, n], g_r.at[j, r], (t, peer)))

    half = out_ref.shape[0]

    def away(i, h):
        return jnp.logical_or(4 * c + i != t, c != h)

    def arrive(j):
        landed(ga.at[j, across], g_s.at[j, 0], g_r.at[j, across])
        sent.append(push(ga.at[j, across], ga.at[j, across], g_s.at[j, 2], g_r.at[j, across], (t, mate)))

    def hop(j, i, h):
        return pltpu.make_async_remote_copy(
            src_ref=pst.at[j, i, h], dst_ref=prec.at[j, t], send_sem=p_s.at[j, i, h],
            recv_sem=p_r.at[j, t], device_id=(4 * c + i, 2 * y + h), device_id_type=MESH,
        )

    arrive(0)
    for j in range(pieces):
        if j + 1 < pieces:
            arrive(j + 1)
        for peer in (mate, diag):
            landed(ga.at[j, peer], g_s.at[j, 0], g_r.at[j, peer])
        part = dot(fct[...], ga[j].reshape(tile, piece)).astype(jnp.bfloat16)
        for i in range(4):
            for h in range(2):
                pst[j, i, h] = part[(2 * i + h) * half : (2 * i + h + 1) * half]
        for i in range(4):
            for h in range(2):
                @pl.when(away(i, h))
                def _():
                    hop(j, i, h).start()

                @pl.when(jnp.logical_not(away(i, h)))
                def _():
                    prec[j, t] = pst[j, i, h]

    for j in range(pieces):
        for step in range(nb):
            @pl.when(jnp.logical_or(t // 4 != c, t != step))
            def _():
                landed(prec.at[j, step], p_s.at[j, 0, 0], p_r.at[j, step])

        result = prec[j, 0].astype(jnp.float32)
        for step in range(1, nb):
            result = result + prec[j, step].astype(jnp.float32)
        out_ref[:, j * piece : (j + 1) * piece] = result
    for j in range(pieces):
        for i in range(4):
            for h in range(2):
                @pl.when(away(i, h))
                def _():
                    hop(j, i, h).wait_send()
    for copy in sent:
        copy.wait_send()


def fused(features, head_weight, labels, pos_index, pair_mask, loss_weight):
    quarter, depth = features.shape
    width = head_weight.shape[1]
    nb = lax.axis_size("blk")
    share = depth // (4 * nb)
    f32, bf16 = jnp.float32, jnp.bfloat16
    dma = pltpu.SemaphoreType.DMA
    vmem = pl.BlockSpec(memory_space=pltpu.VMEM)
    block = (quarter, width)
    small = (8, quarter)
    loss, grad = pl.pallas_call(
        kernel,
        out_shape=(jax.ShapeDtypeStruct((1, quarter), f32), jax.ShapeDtypeStruct((share, width), f32)),
        in_specs=[vmem] * 6,
        out_specs=(vmem, vmem),
        scratch_shapes=[
            pltpu.VMEM((4,) + block, bf16),
            pltpu.VMEM((2,) + block, bf16),
            pltpu.VMEM((4,) + small, f32),
            pltpu.VMEM((2,) + small, f32),
            pltpu.VMEM((4, 4, quarter, 128), bf16),
            pltpu.VMEM((512, 4 * quarter), bf16),
            pltpu.VMEM((4,) + block, f32),
            pltpu.VMEM(block, f32),
            pltpu.VMEM(block, f32),
            pltpu.VMEM((quarter, 128), f32),
            pltpu.VMEM((4,) + small, f32),
            pltpu.VMEM((4, quarter, 128), f32),
            pltpu.VMEM((4,) + small, f32),
            pltpu.VMEM((4, 4) + small, f32),
            pltpu.VMEM((2,) + block, bf16),
            pltpu.VMEM((2,) + block, bf16),
            pltpu.VMEM((2,) + block, bf16),
            pltpu.VMEM((2,) + block, bf16),
            pltpu.VMEM(block, bf16),
            pltpu.VMEM(block, bf16),
            pltpu.VMEM((3, 4, quarter, width // 3), bf16),
            pltpu.VMEM((3, 4, 2, share, width // 3), bf16),
            pltpu.VMEM((3, nb, share, width // 3), bf16),
            dma((3,)), dma((4,)), dma((3,)), dma((4,)),
            dma((2,)), dma((2,)), dma((2,)), dma((2,)),
            dma((3, 4)), dma((4, 4)), dma((2,)), dma((2,)), dma((2,)), dma((2,)), dma(()), dma(()),
            dma((3,)), dma((4,)), dma((3, 3)), dma((3, 4)), dma((3, 4, 2)), dma((3, nb)),
        ],
        compiler_params=pltpu.CompilerParams(
            collective_id=0, has_side_effects=True, vmem_limit_bytes=56 * 1024 * 1024
        ),
    )(features, head_weight, labels[None, :], pos_index.T, loss_weight[None, :], pair_mask)
    return loss[0], grad


def solution(mesh):
    body = fused if mesh.shape["blk"] == 8 and mesh.shape["rows"] == 4 else local
    return jax.shard_map(
        body,
        mesh=mesh,
        in_specs=(
            P(("blk", "rows"), None),
            P(),
            P(("blk", "rows")),
            P(("blk", "rows"), None),
            P("blk", None),
            P(("blk", "rows")),
        ),
        out_specs=(P(("blk", "rows")), P(("blk", "rows"), None)),
        check_vma=False,
    )
```
